512 devices in a mesh: rep: 64 (over x, z_hi, y), ctx: 8 (over z_lo, core).
Axes of the slice: x: 4, y: 8, z: 8 (z_hi: 2, z_lo: 4; z = z_hi * 4 + z_lo), core: 2. Of those that a mesh axis runs over, the one named last changes fastest.
Arguments:
- activations: bfloat16 [64, 1024, 4096], P('rep', 'ctx'), may hold values from -6 to 6
- queries: bfloat16 [64, 1024, 2048], P('rep', 'ctx'), may hold values from -110 to 110
- key_states: bfloat16 [64, 1024, 512], P('rep', 'ctx'), may hold values from -4 to 4
- targets: bfloat16 [64, 1024, 2048], P('rep', 'ctx'), may hold values from -1.5 to 1.5
- value_weight: bfloat16 [64, 4096, 512], P('rep', 'ctx'), may hold values from -5 to 5
- tracker: bfloat16 [64, 4096, 512], P('rep', 'ctx'), may hold values from -5 to 5
- old_gradient: bfloat16 [64, 4096, 512], P('rep', 'ctx'), may hold values from -5 to 5
Outputs:
- new_weight: bfloat16 [64, 4096, 512], P('rep', 'ctx')
- new_tracker: bfloat16 [64, 4096, 512], P('rep', 'ctx')
The draws below stay inside these ranges and needn't reach their ends.
All inputs are finite; a program needn't handle non-finite values.
Results may differ from the reference program's by a relative error of at most 0.0095.
Values may be sent and summed in bfloat16 or wider, within the bound.
A program may use at most 64 MiB of HBM per device.

```python
import jax
import jax.numpy as jnp
from jax import lax

D = 4096
HEADS = 16
KV_HEADS = 4
HEAD_DIM = 128
ROUND = 3
SEQ = 1024
N_REP = 64


def paired_draw(key):
    base = jax.random.fold_in(key, 17)
    key_part, query_part = jax.random.split(base)
    key_rows = jax.random.truncated_normal(key_part, -4.0, 4.0, (N_REP, SEQ, KV_HEADS * HEAD_DIM), jnp.float32)
    query_rows = jax.random.truncated_normal(query_part, -4.0, 4.0, (N_REP, SEQ, HEADS * HEAD_DIM), jnp.float32)
    return (query_rows, key_rows)


def draw_queries(key, part):
    return paired_draw(key)[0].astype(jnp.bfloat16)


def draw_key_states(key, part):
    return paired_draw(key)[1].astype(jnp.bfloat16)


def block_levels(stream_key, extent, cuts, least, largest):
    level = 1.0
    for dim, shards_of in cuts:
        draws = jax.random.uniform(jax.random.fold_in(jax.random.fold_in(stream_key, 6), dim), (shards_of,), jnp.float32, least / len(cuts), largest / len(cuts))
        level = level * jnp.repeat(jnp.exp(draws), extent[dim] // shards_of).reshape((-1,) + (1,) * (len(extent) - 1 - dim))
    return level


def noise(own_key, dims, width, reach, shards=(), held_as=jnp.bfloat16):
    level = block_levels(own_key, dims, shards, -0.22, 0.18) if shards else 1.0
    entries = jax.random.normal(own_key, dims, jnp.float32) * width * level
    return jnp.minimum(jnp.maximum(entries, -reach), reach).astype(held_as)


def setup_inputs(seed: int = 0) -> dict:
    keys = jax.random.split(jax.random.key(seed), 8)
    activations = noise(keys[0], (N_REP, SEQ, D), 1.0, 6.0, ((0, 64), (1, 8)))
    queries = draw_queries(jax.random.fold_in(keys[7], 71), 0)
    key_states = draw_key_states(jax.random.fold_in(keys[7], 71), 0)
    targets = noise(keys[3], (N_REP, SEQ, HEADS * HEAD_DIM), 0.25, 1.5, ((0, 64), (1, 8)))
    value_weight = noise(keys[4], (N_REP, D, KV_HEADS * HEAD_DIM), 1.0, 5.0, ((0, 64), (1, 8)))
    tracker = noise(keys[5], (N_REP, D, KV_HEADS * HEAD_DIM), 1.0, 5.0, ((0, 64), (1, 8)))
    old_gradient = noise(keys[6], (N_REP, D, KV_HEADS * HEAD_DIM), 1.0, 5.0, ((0, 64), (1, 8)))
    return dict(activations=activations, queries=queries, key_states=key_states, targets=targets, value_weight=value_weight, tracker=tracker, old_gradient=old_gradient)


step_size = 0.25
loss_weight = 16.0


def replica_round(operands):
    activations, queries, key_states, targets, weight, tracker, old_gradient = operands
    value_scale = D ** -0.5
    grouping = HEADS // KV_HEADS
    values = (jnp.dot(activations, weight, preferred_element_type=jnp.float32) * value_scale).astype(jnp.bfloat16)
    query_heads = queries.astype(jnp.float32).reshape(SEQ, KV_HEADS, grouping, HEAD_DIM)
    key_heads = key_states.astype(jnp.float32).reshape(SEQ, KV_HEADS, HEAD_DIM)
    value_heads = values.astype(jnp.float32).reshape(SEQ, KV_HEADS, HEAD_DIM)
    scores = jnp.einsum("ikgd,jkd->kgij", query_heads, key_heads) * (HEAD_DIM ** -0.5)
    positions = jnp.arange(SEQ)
    allowed = positions[None, :] <= positions[:, None]
    scores = jnp.where(allowed, scores, -jnp.inf)
    highest = jnp.max(scores, axis=-1, keepdims=True)
    raised = jnp.exp(scores - highest)
    probabilities = (raised / jnp.sum(raised, axis=-1, keepdims=True)).astype(jnp.bfloat16)
    prob_full = probabilities.astype(jnp.float32)
    attended = jnp.einsum("kgij,jkd->ikgd", prob_full, value_heads).reshape(SEQ, HEADS * HEAD_DIM)
    out_cot = (loss_weight * (attended - targets.astype(jnp.float32))).astype(jnp.bfloat16)
    cot_heads = out_cot.astype(jnp.float32).reshape(SEQ, KV_HEADS, grouping, HEAD_DIM)
    value_cot = jnp.einsum("kgij,ikgd->jkd", prob_full, cot_heads).reshape(SEQ, KV_HEADS * HEAD_DIM)
    value_cot16 = value_cot.astype(jnp.bfloat16)
    gradient = jnp.dot(activations.T, value_cot16, preferred_element_type=jnp.float32) * value_scale
    tracker_half = tracker.astype(jnp.float32) + gradient - old_gradient.astype(jnp.float32)
    moved = weight.astype(jnp.float32) - step_size * tracker_half
    return moved, tracker_half


def reference(activations, queries, key_states, targets, value_weight, tracker, old_gradient):
    moved, tracker_half = lax.map(replica_round, (activations, queries, key_states, targets, value_weight, tracker, old_gradient))
    partner = jnp.bitwise_xor(jnp.arange(N_REP, dtype=jnp.int32), jnp.int32(2 ** ROUND))
    new_weight = ((moved + moved[partner]) * 0.5).astype(jnp.bfloat16)
    new_tracker = ((tracker_half + tracker_half[partner]) * 0.5).astype(jnp.bfloat16)
    return new_weight, new_tracker
```

```python
import functools

import jax
import jax.numpy as jnp
from jax import lax
from jax.experimental import pallas as pl
from jax.experimental.pallas import tpu as pltpu
from jax.sharding import PartitionSpec as P

ROUND = 3
STEP = 0.25
LOSS = 16.0
CTX = 8
CHIPS = 4
ROWS = 128
SEQ = 1024
HALF = 512
D = 4096
FEAT = 512
COLS = 512
HD = 128
QB = 256
LOG2E = 1.4426950408889634
F32 = jnp.float32
BF16 = jnp.bfloat16
MESH = pl.DeviceIdType.MESH


def dot(a, b):
    return jnp.dot(a, b, preferred_element_type=F32)


def dot_nt(a, b):
    return lax.dot_general(a, b, (((1,), (1,)), ((), ())), preferred_element_type=F32)


def kernel(
    a_h, q_h, k_h, t_h, w_h, tr_h, og_h,
    nw_ref, nt_ref,
    abuf, qbuf, kbuf, tbuf, wv, trv, ogv, ft, psend, pown, precv, sums, rbuf,
    v, vt, acc, trecv, vc, th, th16, thp, wp,
    a_s, a_r, q_s, q_r, k_s, k_r, t_s, t_r, w_s, w_r, p_s, p_r, r_s, r_r,
    v_s, v_r, c_s, c_r, b_s, b_r, f_s, f_r, x_s, x_r, loc,
):
    me = lax.axis_index("ctx")
    rep = lax.axis_index("rep")
    i = lax.div(me, 2)
    s = lax.rem(me, 2)
    mate = me + 1 - 2 * s
    apart = 1 << ROUND
    peer = rep + apart * (1 - 2 * lax.rem(lax.div(rep, apart), 2))

    def lanes(n, size):
        return pl.ds(pl.multiple_of(n * size, size), size)

    def remote(src, dst, ss, rs, ctx, r=None):
        return pltpu.make_async_remote_copy(
            src_ref=src, dst_ref=dst, send_sem=ss, recv_sem=rs,
            device_id=(rep if r is None else r, ctx), device_id_type=MESH,
        )

    def arrived(ref, sem):
        pltpu.make_async_copy(ref, ref, sem).wait()

    barrier = pltpu.get_barrier_semaphore()
    for k in range(1, CTX):
        pl.semaphore_signal(barrier, inc=1, device_id=(rep, lax.rem(me + k, CTX)), device_id_type=MESH)
    pl.semaphore_signal(barrier, inc=1, device_id=(peer, me), device_id_type=MESH)

    mine = lanes(me, ROWS)
    own = [
        pltpu.make_async_copy(w_h, wv, loc.at[0]),
        pltpu.make_async_copy(a_h.at[:, lanes(me, FEAT)], abuf.at[me], a_r.at[me]),
        pltpu.make_async_copy(q_h.at[:, lanes(me, 2 * HD)], qbuf.at[mine], q_r.at[me]),
        pltpu.make_async_copy(k_h.at[:, lanes(i, HD)], kbuf.at[mine], k_r.at[me]),
        pltpu.make_async_copy(t_h.at[:, lanes(me, 2 * HD)], tbuf.at[mine], t_r.at[me]),
        pltpu.make_async_copy(tr_h, trv, loc.at[1]),
        pltpu.make_async_copy(og_h, ogv, loc.at[2]),
    ]
    for copy in own:
        copy.start()

    pl.semaphore_wait(barrier, CTX)

    sends = []

    def send(*args):
        copy = remote(*args)
        copy.start()
        sends.append(copy)

    order = (4, 3, 5, 2, 6, 1, 7)
    for k in order:
        p = lax.rem(me + k, CTX)
        send(a_h.at[:, lanes(p, FEAT)], abuf.at[me], a_s.at[k], a_r.at[me], p)
    for k in order:
        p = lax.rem(me + k, CTX)
        send(k_h.at[:, lanes(lax.div(p, 2), HD)], kbuf.at[mine], k_s.at[k], k_r.at[me], p)
    for k in order:
        p = lax.rem(me + k, CTX)
        send(q_h.at[:, lanes(p, 2 * HD)], qbuf.at[mine], q_s.at[k], q_r.at[me], p)
    for k in order:
        p = lax.rem(me + k, CTX)
        send(t_h.at[:, lanes(p, 2 * HD)], tbuf.at[mine], t_s.at[k], t_r.at[me], p)

    own[0].wait()
    for m in range(4):
        j = 4 * (1 - s) + m
        arrived(abuf.at[j], a_r.at[j])
        psend[m] = dot(abuf[j], wv[...])
        send(psend.at[m], precv.at[m], p_s.at[m], p_r.at[m], mate)
        ft[:, lanes(j, ROWS)] = abuf[j].T
    for m in range(4):
        j = 4 * s + m
        arrived(abuf.at[j], a_r.at[j])
        pown[m] = dot(abuf[j], wv[...])
        ft[:, lanes(j, ROWS)] = abuf[j].T
    for m in range(4):
        arrived(precv.at[m], p_r.at[m])
        total = pown[m] + precv[m]
        for k in range(CHIPS):
            sums[k, m * ROWS:(m + 1) * ROWS, :] = total[:, k * HD:(k + 1) * HD].astype(BF16)
    for k in (2, 1, 3):
        kc = lax.rem(i + k, CHIPS)
        send(sums.at[kc], rbuf.at[i], r_s.at[k], r_r.at[i], 2 * kc + s)
    send(w_h, wp, w_s.at[0], w_r.at[0], me, peer)
    for k in range(1, CHIPS):
        src = lax.rem(i + k, CHIPS)
        arrived(rbuf.at[src], r_r.at[src])
    for m in range(4):
        rows = slice(m * ROWS, (m + 1) * ROWS)
        total = pown[m, :, lanes(i, HD)] + precv[m, :, lanes(i, HD)]
        for k in range(1, CHIPS):
            total = total + rbuf[lax.rem(i + k, CHIPS), rows, :].astype(F32)
        v[s, rows, :] = (total * D ** -0.5).astype(BF16)
    send(v.at[s], v.at[s], v_s.at[0], v_r.at[0], mate)
    arrived(v.at[1 - s], v_r.at[0])
    for h in range(2):
        vt[:, h * HALF:(h + 1) * HALF] = v[h].T

    for j in range(CTX):
        rows = slice(j * ROWS, (j + 1) * ROWS)
        arrived(kbuf.at[rows], k_r.at[j])
        arrived(qbuf.at[rows], q_r.at[j])
        arrived(tbuf.at[rows], t_r.at[j])
    acc[...] = jnp.zeros_like(acc)
    later = lax.broadcasted_iota(jnp.int32, (QB, QB), 0) > lax.broadcasted_iota(jnp.int32, (QB, QB), 1)

    def head(g, carry):
        cols = lanes(g, HD)
        for b in range(SEQ // QB):
            at = slice(b * QB, (b + 1) * QB)
            upto = (b + 1) * QB
            scores = dot_nt(kbuf[:upto, :], qbuf[at, cols])
            edge = jnp.where(later, -jnp.inf, scores[b * QB:, :])
            scores = jnp.concatenate((scores[:b * QB, :], edge), axis=0) if b else edge
            highest = jnp.max(scores, axis=0, keepdims=True)
            raised = jnp.exp2((scores - highest) * (HD ** -0.5 * LOG2E))
            share = 1.0 / jnp.sum(raised, axis=0, keepdims=True)
            prob = (raised * share).astype(BF16)
            attended = dot(vt[:, :upto], prob).T
            cot = (LOSS * (attended - tbuf[at, cols].astype(F32))).astype(BF16)
            acc[:upto, :] += dot(prob, cot)
        return carry

    lax.fori_loop(0, 2, head, 0)

    half = pl.ds(pl.multiple_of(s * HALF, HALF), HALF)
    other = pl.ds(pl.multiple_of((1 - s) * HALF, HALF), HALF)
    send(acc.at[other], trecv, c_s.at[0], c_r.at[0], mate)
    arrived(trecv, c_r.at[0])
    vc[i, half, :] = (acc[half, :] + trecv[...]).astype(BF16)
    block = vc.at[i, half]
    send(block, block, f_s.at[0], f_r.at[i], mate)
    for k in (2, 1, 3):
        send(block, block, b_s.at[k], b_r.at[i], 2 * lax.rem(i + k, CHIPS) + s)

    own[5].wait()
    own[6].wait()
    for k in range(CHIPS):
        h = lax.rem(i + k, CHIPS)
        if k:
            landed = vc.at[h, half]
            arrived(landed, b_r.at[h])
            send(landed, landed, f_s.at[k], f_r.at[h], mate)
        arrived(vc.at[h, other], f_r.at[h])
        cols = lanes(h, HD)
        gradient = dot(ft[...], vc[h]) * D ** -0.5
        stepped = trv[:, cols].astype(F32) + gradient - ogv[:, cols].astype(F32)
        th[h] = stepped
        th16[h] = stepped.astype(BF16)
        send(th16.at[h], thp.at[h], x_s.at[k], x_r.at[h], me, peer)

    arrived(wp, w_r.at[0])
    for k in range(CHIPS):
        h = lax.rem(i + k, CHIPS)
        cols = lanes(h, HD)
        arrived(thp.at[h], x_r.at[h])
        mixed = (th[h] + thp[h].astype(F32)) * 0.5
        nt_ref[:, cols] = mixed.astype(BF16)
        nw_ref[:, cols] = (
            (wv[:, cols].astype(F32) + wp[:, cols].astype(F32)) * 0.5 - STEP * mixed
        ).astype(BF16)
    for copy in sends:
        copy.wait_send()


def local(activations, queries, key_states, targets, value_weight, tracker, old_gradient):
    dma = lambda n: pltpu.SemaphoreType.DMA((n,))
    shape = jax.ShapeDtypeStruct((FEAT, COLS), BF16)
    new_weight, new_tracker = pl.pallas_call(
        kernel,
        out_shape=(shape, shape),
        in_specs=[pl.BlockSpec(memory_space=pl.ANY)] * 7,
        out_specs=(pl.BlockSpec(memory_space=pltpu.VMEM),) * 2,
        scratch_shapes=[
            pltpu.VMEM((CTX, ROWS, FEAT), BF16),
            pltpu.VMEM((SEQ, 2 * HD), BF16),
            pltpu.VMEM((SEQ, HD), BF16),
            pltpu.VMEM((SEQ, 2 * HD), BF16),
            pltpu.VMEM((FEAT, COLS), BF16),
            pltpu.VMEM((FEAT, COLS), BF16),
            pltpu.VMEM((FEAT, COLS), BF16),
            pltpu.VMEM((FEAT, SEQ), BF16),
            pltpu.VMEM((4, ROWS, COLS), F32),
            pltpu.VMEM((4, ROWS, COLS), F32),
            pltpu.VMEM((4, ROWS, COLS), F32),
            pltpu.VMEM((CHIPS, HALF, HD), BF16),
            pltpu.VMEM((CHIPS, HALF, HD), BF16),
            pltpu.VMEM((2, HALF, HD), BF16),
            pltpu.VMEM((HD, SEQ), BF16),
            pltpu.VMEM((SEQ, HD), F32),
            pltpu.VMEM((HALF, HD), F32),
            pltpu.VMEM((CHIPS, SEQ, HD), BF16),
            pltpu.VMEM((CHIPS, FEAT, HD), F32),
            pltpu.VMEM((CHIPS, FEAT, HD), BF16),
            pltpu.VMEM((CHIPS, FEAT, HD), BF16),
            pltpu.VMEM((FEAT, COLS), BF16),
            dma(8), dma(8), dma(8), dma(8), dma(8), dma(8), dma(8), dma(8),
            dma(1), dma(1), dma(4), dma(4), dma(4), dma(4),
            dma(1), dma(1), dma(1), dma(1), dma(4), dma(4), dma(4), dma(4), dma(4), dma(4), dma(3),
        ],
        compiler_params=pltpu.CompilerParams(
            collective_id=0, has_side_effects=True, vmem_limit_bytes=56 * 1024 * 1024
        ),
    )(
        activations[0], queries[0], key_states[0], targets[0],
        value_weight[0], tracker[0], old_gradient[0],
    )
    return new_weight[None], new_tracker[None]


def solution(mesh):
    spec = P("rep", "ctx", None)
    return jax.shard_map(
        local, mesh=mesh, in_specs=(spec,) * 7, out_specs=(spec, spec), check_vma=False
    )
```

```python
import jax
import jax.numpy as jnp
from jax import lax
from jax.experimental import pallas as pl
from jax.experimental.pallas import tpu as pltpu
from jax.sharding import PartitionSpec as P

ROUND = 3
STEP = 0.25
LOSS = 16.0
CTX = 8
CHIPS = 4
ROWS = 128
SEQ = 1024
HALF = 512
D = 4096
FEAT = 512
COLS = 512
HD = 128
GROUP = 4
QB = 256
LOG2E = 1.4426950408889634
FILL = (2, 1, 1, 0)
F32 = jnp.float32
BF16 = jnp.bfloat16
MESH = pl.DeviceIdType.MESH


def dot(a, b):
    return jnp.dot(a, b, preferred_element_type=F32)


def dot_nt(a, b):
    return lax.dot_general(a, b, (((1,), (1,)), ((), ())), preferred_element_type=F32)


def kernel(
    a_h, q_h, k_h, t_h, w_h, tr_h, og_h,
    nw_ref, nt_ref,
    abuf, qbuf, kbuf, tbuf, wv, trv, ogv, ft, part, pin, sums, rbuf,
    v, vt, pt, cot, cross, trecv, vc, th, th16, thp, wp,
    a_s, a_r, q_s, q_r, k_s, k_r, t_s, t_r, w_s, w_r, p_s, p_r, r_s, r_r,
    v_s, v_r, c_s, c_r, g_s, g_r, m_s, m_r, x_s, x_r, loc,
):
    me = lax.axis_index("ctx")
    rep = lax.axis_index("rep")
    i = lax.div(me, 2)
    s = lax.rem(me, 2)
    p = lax.div(me, 4)
    a = lax.rem(i, 2)
    e = lax.rem(me, 4)
    q = 1 - p
    mate = me + 1 - 2 * s
    apart = 1 << ROUND
    peer = rep + apart * (1 - 2 * lax.rem(lax.div(rep, apart), 2))

    def dev(x, aa, ss):
        return 4 * x + 2 * aa + ss

    def lanes(n, size):
        return pl.ds(pl.multiple_of(n * size, size), size)

    def remote(src, dst, ss, rs, ctx, r=None):
        return pltpu.make_async_remote_copy(
            src_ref=src, dst_ref=dst, send_sem=ss, recv_sem=rs,
            device_id=(rep if r is None else r, ctx), device_id_type=MESH,
        )

    def arrived(ref, sem):
        pltpu.make_async_copy(ref, ref, sem).wait()

    barrier = pltpu.get_barrier_semaphore()
    pl.semaphore_signal(barrier, inc=1, device_id=(peer, me), device_id_type=MESH)
    for k in range(1, CTX):
        pl.semaphore_signal(barrier, inc=1, device_id=(rep, lax.rem(me + k, CTX)), device_id_type=MESH)

    mine = lanes(me, ROWS)
    here = lanes(e, ROWS)
    own = [
        pltpu.make_async_copy(w_h, wv, loc.at[0]),
        pltpu.make_async_copy(a_h.at[:, lanes(me, FEAT)], abuf.at[me], a_r.at[me]),
        pltpu.make_async_copy(k_h.at[:, lanes(e, HD)], kbuf.at[mine], k_r.at[me]),
        pltpu.make_async_copy(q_h.at[:, lanes(e, GROUP * HD)], qbuf.at[here], q_r.at[e]),
        pltpu.make_async_copy(t_h.at[:, lanes(e, GROUP * HD)], tbuf.at[here], t_r.at[e]),
        pltpu.make_async_copy(tr_h, trv, loc.at[1]),
        pltpu.make_async_copy(og_h, ogv, loc.at[2]),
    ]
    for copy in own:
        copy.start()

    pl.semaphore_wait(barrier, CTX)

    sends = []

    def send(*args):
        copy = remote(*args)
        copy.start()
        sends.append(copy)

    near = [dev(p, 1 - a, s), dev(p, 1 - a, 1 - s), mate]
    far = [dev(q, 1 - a, s), dev(q, 1 - a, 1 - s), dev(q, a, s), dev(q, a, 1 - s)]
    for n, to in enumerate(far + near):
        send(a_h.at[:, lanes(to, FEAT)], abuf.at[me], a_s.at[n], a_r.at[me], to)
    k_out = []
    for n, to in enumerate(far):
        k_out.append(remote(k_h.at[:, lanes(lax.rem(to, 4), HD)], kbuf.at[mine], k_s.at[n], k_r.at[me], to))

    @pl.when(p == 0)
    def _():
        for copy in k_out:
            copy.start()

    for n, to in enumerate(near):
        send(k_h.at[:, lanes(lax.rem(to, 4), HD)], kbuf.at[mine], k_s.at[4 + n], k_r.at[me], to)
    for n, to in enumerate(near):
        send(q_h.at[:, lanes(lax.rem(to, 4), GROUP * HD)], qbuf.at[here], q_s.at[n], q_r.at[e], to)
    for n, to in enumerate(near):
        send(t_h.at[:, lanes(lax.rem(to, 4), GROUP * HD)], tbuf.at[here], t_s.at[n], t_r.at[e], to)

    own[0].wait()
    for x, swap in ((p, 0), (q, 1)):
        rows = lanes(x, HALF)
        for m in range(4):
            j = 4 * x + m
            arrived(abuf.at[j], a_r.at[j])
            product = dot(abuf[j], wv[...])
            for h in range(4):
                part[h, lanes(j, ROWS), :] = product[:, h * HD:(h + 1) * HD]
            if m % 2:
                quarter = lanes(2 * x + m // 2, 2 * ROWS)
                for b in range(2):
                    n = 4 * swap + 2 * (m // 2) + b
                    send(part.at[2 * b + 1 - s, quarter], pin.at[b, quarter], p_s.at[n], p_r.at[n], mate)
        for m in range(4):
            j = 4 * x + m
            ft[:, lanes(j, ROWS)] = abuf[j].T
        for m in range(2):
            quarter = lanes(2 * x + m, 2 * ROWS)
            for b in range(2):
                n = 4 * swap + 2 * m + b
                arrived(pin.at[b, quarter], p_r.at[n])
                sums[x, b, m * 2 * ROWS:(m + 1) * 2 * ROWS, :] = (
                    part[2 * b + s, quarter, :] + pin[b, quarter, :]
                ).astype(BF16)
        if swap == 0:
            send(sums.at[p, 1 - a], rbuf.at[i], r_s.at[0], r_r.at[i], dev(p, 1 - a, s))
        else:
            send(sums.at[q, 1 - a], rbuf.at[i], r_s.at[1], r_r.at[i], dev(q, 1 - a, s))
            send(sums.at[q, a], rbuf.at[i], r_s.at[2], r_r.at[i], dev(q, a, s))

    chunk = [0]

    def fill(n):
        for _ in range(n):
            rows = pl.ds(chunk[0] * ROWS, ROWS)
            send(w_h.at[rows], wp.at[rows], w_s.at[chunk[0]], w_r.at[chunk[0]], me, peer)
            chunk[0] += 1

    fill(FILL[0])

    for n in range(4):
        rows = pl.ds(n * ROWS, ROWS)
        arrived(qbuf.at[rows], q_r.at[n])
    later = lax.broadcasted_iota(jnp.int32, (QB, QB), 0) > lax.broadcasted_iota(jnp.int32, (QB, QB), 1)

    def softmax(base):
        def head(g, carry):
            for b in range(HALF // QB):
                upto = base + (b + 1) * QB
                scores = dot_nt(kbuf[:upto, :], qbuf[b * QB:(b + 1) * QB, lanes(g, HD)])
                edge = jnp.where(later, -jnp.inf, scores[upto - QB:, :])
                scores = jnp.concatenate((scores[:upto - QB, :], edge), axis=0) if upto > QB else edge
                highest = jnp.max(scores, axis=0, keepdims=True)
                raised = jnp.exp2((scores - highest) * (HD ** -0.5 * LOG2E))
                share = 1.0 / jnp.sum(raised, axis=0, keepdims=True)
                cols = lanes(2 * g + b, QB)
                pt[:upto, cols] = (raised * share).astype(BF16)
                if upto < base + HALF:
                    pt[upto:base + HALF, cols] = jnp.zeros((base + HALF - upto, QB), BF16)
            return carry

        lax.fori_loop(0, GROUP, head, 0)

    for j in range(4):
        arrived(kbuf.at[pl.ds(j * ROWS, ROWS)], k_r.at[j])

    @pl.when(p == 0)
    def _():
        softmax(0)

    @pl.when(p == 1)
    def _():
        for j in range(4, CTX):
            arrived(kbuf.at[pl.ds(j * ROWS, ROWS)], k_r.at[j])
        softmax(HALF)

    for other in (2 * p + 1 - a, 2 * q + a, 2 * q + 1 - a):
        arrived(rbuf.at[other], r_r.at[other])
    for m in range(2):
        rows = slice(m * 2 * ROWS, (m + 1) * 2 * ROWS)
        quarter = lanes(2 * p + m, 2 * ROWS)
        total = part[e, quarter, :] + pin[a, quarter, :]
        for other in (2 * p + 1 - a, 2 * q + a, 2 * q + 1 - a):
            total = total + rbuf[other, rows, :].astype(F32)
        v[p, rows, :] = (total * D ** -0.5).astype(BF16)
    onward = remote(v.at[0], v.at[0], v_s.at[0], v_r.at[0], dev(1, a, s))

    @pl.when(p == 0)
    def _():
        onward.start()

    fill(FILL[1])
    vt[:, lanes(p, HALF)] = v[p].T
    for n in range(4):
        rows = pl.ds(n * ROWS, ROWS)
        arrived(tbuf.at[rows], t_r.at[n])

    def attend(base):
        def head(g, carry):
            for b in range(HALF // QB):
                upto = base + (b + 1) * QB
                n = lanes(2 * g + b, QB)
                attended = dot(vt[:, :upto], pt[:upto, n]).T
                wanted = tbuf[b * QB:(b + 1) * QB, lanes(g, HD)].astype(F32)
                cot[n, :] = (LOSS * (attended - wanted)).astype(BF16)
            return carry

        lax.fori_loop(0, GROUP, head, 0)

    @pl.when(p == 0)
    def _():
        attend(0)
        terms = dot(pt[:HALF, :], cot[...])
        arrived(trecv, c_r.at[0])
        vc[e, :HALF, :] = (terms + trecv[...].astype(F32)).astype(BF16)

    back = remote(cross, trecv, c_s.at[0], c_r.at[0], dev(0, a, s))

    @pl.when(p == 1)
    def _():
        arrived(v.at[0], v_r.at[0])
        vt[:, :HALF] = v[0].T
        attend(HALF)
        cross[...] = dot(pt[:HALF, :], cot[...]).astype(BF16)
        back.start()
        vc[e, HALF:, :] = dot(pt[HALF:, :], cot[...]).astype(BF16)

    def block(x, aa, ss):
        return vc.at[2 * aa + ss, lanes(x, HALF)]

    send(block(p, a, s), block(p, a, s), g_s.at[0], g_r.at[i], dev(q, a, s))
    send(block(p, a, s), block(p, a, s), g_s.at[1], g_r.at[i], dev(p, 1 - a, s))
    send(block(p, a, s), block(p, a, s), m_s.at[0], m_r.at[i], mate)
    fill(FILL[2])

    own[5].wait()
    own[6].wait()

    def gradient(n, h):
        cols = lanes(h, HD)
        grad = dot(ft[...], vc[h]) * D ** -0.5
        stepped = trv[:, cols].astype(F32) + grad - ogv[:, cols].astype(F32)
        th[h] = stepped
        th16[h] = stepped.astype(BF16)
        send(th16.at[h], thp.at[h], x_s.at[n], x_r.at[h], me, peer)

    def landed(x, aa):
        arrived(block(x, aa, s), g_r.at[2 * x + aa])

    def passed(x, aa):
        arrived(block(x, aa, 1 - s), m_r.at[2 * x + aa])

    def forward(n, x, aa):
        send(block(x, aa, s), block(x, aa, s), m_s.at[n], m_r.at[2 * x + aa], mate)

    landed(q, a)
    send(block(q, a, s), block(q, a, s), g_s.at[2], g_r.at[2 * q + a], dev(p, 1 - a, s))
    forward(1, q, a)
    gradient(0, e)
    landed(p, 1 - a)
    forward(2, p, 1 - a)
    passed(p, a)
    passed(q, a)
    gradient(1, 2 * a + 1 - s)
    landed(q, 1 - a)
    forward(3, q, 1 - a)
    gradient(2, 2 * (1 - a) + s)
    passed(p, 1 - a)
    passed(q, 1 - a)
    gradient(3, 2 * (1 - a) + 1 - s)
    fill(FILL[3])

    for n in range(4):
        rows = pl.ds(n * ROWS, ROWS)
        arrived(wp.at[rows], w_r.at[n])
    for h in (e, 2 * a + 1 - s, 2 * (1 - a) + s, 2 * (1 - a) + 1 - s):
        cols = lanes(h, HD)
        arrived(thp.at[h], x_r.at[h])
        mixed = (th[h] + thp[h].astype(F32)) * 0.5
        nt_ref[:, cols] = mixed.astype(BF16)
        nw_ref[:, cols] = (
            (wv[:, cols].astype(F32) + wp[:, cols].astype(F32)) * 0.5 - STEP * mixed
        ).astype(BF16)
    for copy in sends:
        copy.wait_send()

    @pl.when(p == 0)
    def _():
        onward.wait_send()
        for copy in k_out:
            copy.wait_send()

    @pl.when(p == 1)
    def _():
        back.wait_send()


def local(activations, queries, key_states, targets, value_weight, tracker, old_gradient):
    dma = lambda n: pltpu.SemaphoreType.DMA((n,))
    shape = jax.ShapeDtypeStruct((FEAT, COLS), BF16)
    new_weight, new_tracker = pl.pallas_call(
        kernel,
        out_shape=(shape, shape),
        in_specs=[pl.BlockSpec(memory_space=pl.ANY)] * 7,
        out_specs=(pl.BlockSpec(memory_space=pltpu.VMEM),) * 2,
        scratch_shapes=[
            pltpu.VMEM((CTX, ROWS, FEAT), BF16),
            pltpu.VMEM((HALF, GROUP * HD), BF16),
            pltpu.VMEM((SEQ, HD), BF16),
            pltpu.VMEM((HALF, GROUP * HD), BF16),
            pltpu.VMEM((FEAT, COLS), BF16),
            pltpu.VMEM((FEAT, COLS), BF16),
            pltpu.VMEM((FEAT, COLS), BF16),
            pltpu.VMEM((FEAT, SEQ), BF16),
            pltpu.VMEM((4, SEQ, HD), F32),
            pltpu.VMEM((2, SEQ, HD), F32),
            pltpu.VMEM((2, 2, HALF, HD), BF16),
            pltpu.VMEM((CHIPS, HALF, HD), BF16),
            pltpu.VMEM((2, HALF, HD), BF16),
            pltpu.VMEM((HD, SEQ), BF16),
            pltpu.VMEM((SEQ, GROUP * HALF), BF16),
            pltpu.VMEM((GROUP * HALF, HD), BF16),
            pltpu.VMEM((HALF, HD), BF16),
            pltpu.VMEM((HALF, HD), BF16),
            pltpu.VMEM((4, SEQ, HD), BF16),
            pltpu.VMEM((4, FEAT, HD), F32),
            pltpu.VMEM((4, FEAT, HD), BF16),
            pltpu.VMEM((4, FEAT, HD), BF16),
            pltpu.VMEM((FEAT, COLS), BF16),
            dma(7), dma(8), dma(3), dma(4), dma(7), dma(8), dma(3), dma(4),
            dma(4), dma(4), dma(8), dma(8), dma(3), dma(4),
            dma(1), dma(1), dma(1), dma(1), dma(3), dma(4), dma(4), dma(4), dma(4), dma(4), dma(3),
        ],
        compiler_params=pltpu.CompilerParams(
            collective_id=0, has_side_effects=True, vmem_limit_bytes=56 * 1024 * 1024
        ),
    )(
        activations[0], queries[0], key_states[0], targets[0],
        value_weight[0], tracker[0], old_gradient[0],
    )
    return new_weight[None], new_tracker[None]


def solution(mesh):
    spec = P("rep", "ctx", None)
    return jax.shard_map(
        local, mesh=mesh, in_specs=(spec,) * 7, out_specs=(spec, spec), check_vma=False
    )
```

```python
import jax
import jax.numpy as jnp
from jax import lax
from jax.experimental import pallas as pl
from jax.experimental.pallas import tpu as pltpu
from jax.sharding import PartitionSpec as P

ROUND = 3
STEP = 0.25
LOSS = 16.0
CTX = 8
CHIPS = 4
ROWS = 128
SEQ = 1024
HALF = 512
D = 4096
FEAT = 512
COLS = 512
HD = 128
GROUP = 4
QB = 256
LOG2E = 1.4426950408889634
FILL = (1, 2, 1, 0)
F32 = jnp.float32
BF16 = jnp.bfloat16
MESH = pl.DeviceIdType.MESH


def dot(a, b):
    return jnp.dot(a, b, preferred_element_type=F32)


def dot_nt(a, b):
    return lax.dot_general(a, b, (((1,), (1,)), ((), ())), preferred_element_type=F32)


def kernel(
    a_h, q_h, k_h, t_h, w_h, tr_h, og_h,
    th_out, thp_out, wp_out,
    abuf, qbuf, kbuf, tbuf, wv, trv, ogv, ft, part, pin, sums, rbuf,
    v, vt, pt, cot, cross, trecv, vc, th, th16,
    a_s, a_r, q_s, q_r, k_s, k_r, t_s, t_r, w_s, w_r, p_s, p_r, r_s, r_r,
    v_s, v_r, c_s, c_r, g_s, g_r, m_s, m_r, x_s, x_r, loc,
):
    me = lax.axis_index("ctx")
    rep = lax.axis_index("rep")
    i = lax.div(me, 2)
    s = lax.rem(me, 2)
    p = lax.div(me, 4)
    a = lax.rem(i, 2)
    e = lax.rem(me, 4)
    q = 1 - p
    mate = me + 1 - 2 * s
    apart = 1 << ROUND
    peer = rep + apart * (1 - 2 * lax.rem(lax.div(rep, apart), 2))

    def dev(x, aa, ss):
        return 4 * x + 2 * aa + ss

    def lanes(n, size):
        return pl.ds(pl.multiple_of(n * size, size), size)

    def remote(src, dst, ss, rs, ctx, r=None):
        return pltpu.make_async_remote_copy(
            src_ref=src, dst_ref=dst, send_sem=ss, recv_sem=rs,
            device_id=(rep if r is None else r, ctx), device_id_type=MESH,
        )

    def arrived(ref, sem):
        pltpu.make_async_copy(ref, ref, sem).wait()

    barrier = pltpu.get_barrier_semaphore()
    pl.semaphore_signal(barrier, inc=1, device_id=(peer, me), device_id_type=MESH)
    for k in range(1, CTX):
        pl.semaphore_signal(barrier, inc=1, device_id=(rep, lax.rem(me + k, CTX)), device_id_type=MESH)

    mine = lanes(me, ROWS)
    here = lanes(e, ROWS)
    own = [
        pltpu.make_async_copy(w_h, wv, loc.at[0]),
        pltpu.make_async_copy(a_h.at[:, lanes(me, FEAT)], abuf.at[me], a_r.at[me]),
        pltpu.make_async_copy(k_h.at[:, lanes(e, HD)], kbuf.at[mine], k_r.at[me]),
        pltpu.make_async_copy(q_h.at[:, lanes(e, GROUP * HD)], qbuf.at[here], q_r.at[e]),
        pltpu.make_async_copy(t_h.at[:, lanes(e, GROUP * HD)], tbuf.at[here], t_r.at[e]),
        pltpu.make_async_copy(tr_h, trv, loc.at[1]),
        pltpu.make_async_copy(og_h, ogv, loc.at[2]),
    ]
    for copy in own:
        copy.start()

    pl.semaphore_wait(barrier, CTX)

    sends = []

    def send(*args):
        copy = remote(*args)
        copy.start()
        sends.append(copy)

    near = [dev(p, 1 - a, s), dev(p, 1 - a, 1 - s), mate]
    far = [dev(q, 1 - a, s), dev(q, 1 - a, 1 - s), dev(q, a, s), dev(q, a, 1 - s)]
    for n, to in enumerate(far + near):
        send(a_h.at[:, lanes(to, FEAT)], abuf.at[me], a_s.at[n], a_r.at[me], to)
    k_out = []
    for n, to in enumerate(far):
        k_out.append(remote(k_h.at[:, lanes(lax.rem(to, 4), HD)], kbuf.at[mine], k_s.at[n], k_r.at[me], to))

    @pl.when(p == 0)
    def _():
        for copy in k_out:
            copy.start()

    for n, to in enumerate(near):
        send(k_h.at[:, lanes(lax.rem(to, 4), HD)], kbuf.at[mine], k_s.at[4 + n], k_r.at[me], to)
    for n, to in enumerate(near):
        send(q_h.at[:, lanes(lax.rem(to, 4), GROUP * HD)], qbuf.at[here], q_s.at[n], q_r.at[e], to)
    own[0].wait()
    for x, swap in ((p, 0), (q, 1)):
        rows = lanes(x, HALF)
        for m in range(4):
            j = 4 * x + m
            arrived(abuf.at[j], a_r.at[j])
            product = dot(abuf[j], wv[...])
            for h in range(4):
                part[h, lanes(j, ROWS), :] = product[:, h * HD:(h + 1) * HD]
            if m % 2:
                quarter = lanes(2 * x + m // 2, 2 * ROWS)
                for b in range(2):
                    n = 4 * swap + 2 * (m // 2) + b
                    send(part.at[2 * b + 1 - s, quarter], pin.at[b, quarter], p_s.at[n], p_r.at[n], mate)
        for m in range(4):
            j = 4 * x + m
            ft[:, lanes(j, ROWS)] = abuf[j].T
        for m in range(2):
            quarter = lanes(2 * x + m, 2 * ROWS)
            for b in range(2):
                n = 4 * swap + 2 * m + b
                arrived(pin.at[b, quarter], p_r.at[n])
                sums[x, b, m * 2 * ROWS:(m + 1) * 2 * ROWS, :] = (
                    part[2 * b + s, quarter, :] + pin[b, quarter, :]
                ).astype(BF16)
        if swap == 0:
            send(sums.at[p, 1 - a], rbuf.at[i], r_s.at[0], r_r.at[i], dev(p, 1 - a, s))
        else:
            send(sums.at[q, 1 - a], rbuf.at[i], r_s.at[1], r_r.at[i], dev(q, 1 - a, s))
            send(sums.at[q, a], rbuf.at[i], r_s.at[2], r_r.at[i], dev(q, a, s))

    chunk = [0]

    def fill(n):
        for _ in range(n):
            rows = pl.ds(chunk[0] * ROWS, ROWS)
            send(w_h.at[rows], wp_out.at[rows], w_s.at[chunk[0]], w_r.at[chunk[0]], me, peer)
            chunk[0] += 1

    for n, to in enumerate(near):
        send(t_h.at[:, lanes(lax.rem(to, 4), GROUP * HD)], tbuf.at[here], t_s.at[n], t_r.at[e], to)
    fill(FILL[0])

    for n in range(4):
        rows = pl.ds(n * ROWS, ROWS)
        arrived(qbuf.at[rows], q_r.at[n])
    later = lax.broadcasted_iota(jnp.int32, (QB, QB), 0) > lax.broadcasted_iota(jnp.int32, (QB, QB), 1)

    def softmax(base):
        def head(g, carry):
            for b in range(HALF // QB):
                upto = base + (b + 1) * QB
                scores = dot_nt(kbuf[:upto, :], qbuf[b * QB:(b + 1) * QB, lanes(g, HD)])
                edge = jnp.where(later, -jnp.inf, scores[upto - QB:, :])
                scores = jnp.concatenate((scores[:upto - QB, :], edge), axis=0) if upto > QB else edge
                highest = jnp.max(scores, axis=0, keepdims=True)
                raised = jnp.exp2((scores - highest) * (HD ** -0.5 * LOG2E))
                share = 1.0 / jnp.sum(raised, axis=0, keepdims=True)
                cols = lanes(2 * g + b, QB)
                pt[:upto, cols] = (raised * share).astype(BF16)
                if upto < base + HALF:
                    pt[upto:base + HALF, cols] = jnp.zeros((base + HALF - upto, QB), BF16)
            return carry

        lax.fori_loop(0, GROUP, head, 0)

    for j in range(4):
        arrived(kbuf.at[pl.ds(j * ROWS, ROWS)], k_r.at[j])

    @pl.when(p == 0)
    def _():
        softmax(0)

    @pl.when(p == 1)
    def _():
        for j in range(4, CTX):
            arrived(kbuf.at[pl.ds(j * ROWS, ROWS)], k_r.at[j])
        softmax(HALF)

    for other in (2 * p + 1 - a, 2 * q + a, 2 * q + 1 - a):
        arrived(rbuf.at[other], r_r.at[other])
    for m in range(2):
        rows = slice(m * 2 * ROWS, (m + 1) * 2 * ROWS)
        quarter = lanes(2 * p + m, 2 * ROWS)
        total = part[e, quarter, :] + pin[a, quarter, :]
        for other in (2 * p + 1 - a, 2 * q + a, 2 * q + 1 - a):
            total = total + rbuf[other, rows, :].astype(F32)
        v[p, rows, :] = (total * D ** -0.5).astype(BF16)
    onward = remote(v.at[0], v.at[0], v_s.at[0], v_r.at[0], dev(1, a, s))

    @pl.when(p == 0)
    def _():
        onward.start()

    fill(FILL[1])
    vt[:, lanes(p, HALF)] = v[p].T
    for n in range(4):
        rows = pl.ds(n * ROWS, ROWS)
        arrived(tbuf.at[rows], t_r.at[n])

    def attend(base):
        def head(g, carry):
            for b in range(HALF // QB):
                upto = base + (b + 1) * QB
                n = lanes(2 * g + b, QB)
                attended = dot(vt[:, :upto], pt[:upto, n]).T
                wanted = tbuf[b * QB:(b + 1) * QB, lanes(g, HD)].astype(F32)
                cot[n, :] = (LOSS * (attended - wanted)).astype(BF16)
            return carry

        lax.fori_loop(0, GROUP, head, 0)

    @pl.when(p == 0)
    def _():
        attend(0)
        terms = dot(pt[:HALF, :], cot[...])
        arrived(trecv, c_r.at[0])
        vc[e, :HALF, :] = (terms + trecv[...].astype(F32)).astype(BF16)

    back = remote(cross, trecv, c_s.at[0], c_r.at[0], dev(0, a, s))

    @pl.when(p == 1)
    def _():
        arrived(v.at[0], v_r.at[0])
        vt[:, :HALF] = v[0].T
        attend(HALF)
        cross[...] = dot(pt[:HALF, :], cot[...]).astype(BF16)
        back.start()
        vc[e, HALF:, :] = dot(pt[HALF:, :], cot[...]).astype(BF16)

    def block(x, aa, ss):
        return vc.at[2 * aa + ss, lanes(x, HALF)]

    send(block(p, a, s), block(p, a, s), g_s.at[0], g_r.at[i], dev(q, a, s))
    send(block(p, a, s), block(p, a, s), g_s.at[1], g_r.at[i], dev(p, 1 - a, s))
    send(block(p, a, s), block(p, a, s), m_s.at[0], m_r.at[i], mate)
    fill(FILL[2])

    own[5].wait()
    own[6].wait()

    kept = []

    def gradient(n, h):
        cols = lanes(h, HD)
        grad = dot(ft[...], vc[h]) * D ** -0.5
        stepped = trv[:, cols].astype(F32) + grad - ogv[:, cols].astype(F32)
        th[h] = stepped
        th16[h] = stepped.astype(BF16)
        send(th16.at[h], thp_out.at[:, cols], x_s.at[n], x_r.at[n], me, peer)
        keep = pltpu.make_async_copy(th.at[h], th_out.at[:, cols], loc.at[3 + n])
        keep.start()
        kept.append(keep)

    def landed(x, aa):
        arrived(block(x, aa, s), g_r.at[2 * x + aa])

    def passed(x, aa):
        arrived(block(x, aa, 1 - s), m_r.at[2 * x + aa])

    def forward(n, x, aa):
        send(block(x, aa, s), block(x, aa, s), m_s.at[n], m_r.at[2 * x + aa], mate)

    landed(q, a)
    send(block(q, a, s), block(q, a, s), g_s.at[2], g_r.at[2 * q + a], dev(p, 1 - a, s))
    forward(1, q, a)
    gradient(0, e)
    landed(p, 1 - a)
    forward(2, p, 1 - a)
    passed(p, a)
    passed(q, a)
    gradient(1, 2 * a + 1 - s)
    landed(q, 1 - a)
    forward(3, q, 1 - a)
    gradient(2, 2 * (1 - a) + s)
    passed(p, 1 - a)
    passed(q, 1 - a)
    gradient(3, 2 * (1 - a) + 1 - s)
    fill(FILL[3])

    for n in range(4):
        rows = pl.ds(n * ROWS, ROWS)
        arrived(wp_out.at[rows], w_r.at[n])
    for n, h in enumerate((e, 2 * a + 1 - s, 2 * (1 - a) + s, 2 * (1 - a) + 1 - s)):
        kept[n].wait()
        arrived(thp_out.at[:, lanes(h, HD)], x_r.at[n])
    for copy in sends:
        copy.wait_send()

    @pl.when(p == 0)
    def _():
        onward.wait_send()
        for copy in k_out:
            copy.wait_send()

    @pl.when(p == 1)
    def _():
        back.wait_send()


def local(activations, queries, key_states, targets, value_weight, tracker, old_gradient):
    dma = lambda n: pltpu.SemaphoreType.DMA((n,))
    half = jax.ShapeDtypeStruct((FEAT, COLS), BF16)
    th, peer_th, peer_weight = pl.pallas_call(
        kernel,
        out_shape=(jax.ShapeDtypeStruct((FEAT, COLS), F32), half, half),
        in_specs=[pl.BlockSpec(memory_space=pl.ANY)] * 7,
        out_specs=(pl.BlockSpec(memory_space=pl.ANY),) * 3,
        scratch_shapes=[
            pltpu.VMEM((CTX, ROWS, FEAT), BF16),
            pltpu.VMEM((HALF, GROUP * HD), BF16),
            pltpu.VMEM((SEQ, HD), BF16),
            pltpu.VMEM((HALF, GROUP * HD), BF16),
            pltpu.VMEM((FEAT, COLS), BF16),
            pltpu.VMEM((FEAT, COLS), BF16),
            pltpu.VMEM((FEAT, COLS), BF16),
            pltpu.VMEM((FEAT, SEQ), BF16),
            pltpu.VMEM((4, SEQ, HD), F32),
            pltpu.VMEM((2, SEQ, HD), F32),
            pltpu.VMEM((2, 2, HALF, HD), BF16),
            pltpu.VMEM((CHIPS, HALF, HD), BF16),
            pltpu.VMEM((2, HALF, HD), BF16),
            pltpu.VMEM((HD, SEQ), BF16),
            pltpu.VMEM((SEQ, GROUP * HALF), BF16),
            pltpu.VMEM((GROUP * HALF, HD), BF16),
            pltpu.VMEM((HALF, HD), BF16),
            pltpu.VMEM((HALF, HD), BF16),
            pltpu.VMEM((4, SEQ, HD), BF16),
            pltpu.VMEM((4, FEAT, HD), F32),
            pltpu.VMEM((4, FEAT, HD), BF16),
            dma(7), dma(8), dma(3), dma(4), dma(7), dma(8), dma(3), dma(4),
            dma(4), dma(4), dma(8), dma(8), dma(3), dma(4),
            dma(1), dma(1), dma(1), dma(1), dma(3), dma(4), dma(4), dma(4), dma(4), dma(4), dma(7),
        ],
        compiler_params=pltpu.CompilerParams(
            collective_id=0, has_side_effects=True, vmem_limit_bytes=56 * 1024 * 1024
        ),
    )(
        activations[0], queries[0], key_states[0], targets[0],
        value_weight[0], tracker[0], old_gradient[0],
    )
    mixed = (th + peer_th.astype(F32)) * 0.5
    weights = (value_weight[0].astype(F32) + peer_weight.astype(F32)) * 0.5
    return (weights - STEP * mixed).astype(BF16)[None], mixed.astype(BF16)[None]


def solution(mesh):
    spec = P("rep", "ctx", None)
    return jax.shard_map(
        local, mesh=mesh, in_specs=(spec,) * 7, out_specs=(spec, spec), check_vma=False
    )
```

```python
import jax
import jax.numpy as jnp
from jax import lax
from jax.experimental import pallas as pl
from jax.experimental.pallas import tpu as pltpu
from jax.sharding import PartitionSpec as P

ROUND = 3
STEP = 0.25
LOSS = 16.0
CTX = 8
CHIPS = 4
ROWS = 128
SEQ = 1024
HALF = 512
D = 4096
FEAT = 512
COLS = 512
HD = 128
GROUP = 4
QB = 256
LOG2E = 1.4426950408889634
FILL = (1, 2, 1, 0)
F32 = jnp.float32
BF16 = jnp.bfloat16
MESH = pl.DeviceIdType.MESH


def dot(a, b):
    return jnp.dot(a, b, preferred_element_type=F32)


def dot_nt(a, b):
    return lax.dot_general(a, b, (((1,), (1,)), ((), ())), preferred_element_type=F32)


def kernel(
    a_h, q_h, k_h, t_h, w_h, tr_h, og_h,
    th_out, thp_out, wp_out,
    abuf, qbuf, kbuf, tbuf, wv, trv, ogv, ft, part, pout, pin, sums, rbuf,
    v, vt, pt, cot, cross, trecv, vc, th, th16,
    a_s, a_r, q_s, q_r, k_s, k_r, t_s, t_r, w_s, w_r, p_s, p_r, r_s, r_r,
    v_s, v_r, c_s, c_r, g_s, g_r, m_s, m_r, x_s, x_r, loc,
):
    me = lax.axis_index("ctx")
    rep = lax.axis_index("rep")
    i = lax.div(me, 2)
    s = lax.rem(me, 2)
    p = lax.div(me, 4)
    a = lax.rem(i, 2)
    e = lax.rem(me, 4)
    q = 1 - p
    mate = me + 1 - 2 * s
    apart = 1 << ROUND
    peer = rep + apart * (1 - 2 * lax.rem(lax.div(rep, apart), 2))

    def dev(x, aa, ss):
        return 4 * x + 2 * aa + ss

    def lanes(n, size):
        return pl.ds(pl.multiple_of(n * size, size), size)

    def remote(src, dst, ss, rs, ctx, r=None):
        return pltpu.make_async_remote_copy(
            src_ref=src, dst_ref=dst, send_sem=ss, recv_sem=rs,
            device_id=(rep if r is None else r, ctx), device_id_type=MESH,
        )

    def arrived(ref, sem):
        pltpu.make_async_copy(ref, ref, sem).wait()

    barrier = pltpu.get_barrier_semaphore()
    pl.semaphore_signal(barrier, inc=1, device_id=(peer, me), device_id_type=MESH)
    for k in range(1, CTX):
        pl.semaphore_signal(barrier, inc=1, device_id=(rep, lax.rem(me + k, CTX)), device_id_type=MESH)

    mine = lanes(me, ROWS)
    here = lanes(e, ROWS)
    own = [
        pltpu.make_async_copy(w_h, wv, loc.at[0]),
        pltpu.make_async_copy(a_h.at[:, lanes(me, FEAT)], abuf.at[me], a_r.at[me]),
        pltpu.make_async_copy(k_h.at[:, lanes(e, HD)], kbuf.at[mine], k_r.at[me]),
        pltpu.make_async_copy(q_h.at[:, lanes(e, GROUP * HD)], qbuf.at[here], q_r.at[e]),
        pltpu.make_async_copy(t_h.at[:, lanes(e, GROUP * HD)], tbuf.at[here], t_r.at[e]),
        pltpu.make_async_copy(tr_h, trv, loc.at[1]),
        pltpu.make_async_copy(og_h, ogv, loc.at[2]),
    ]
    for copy in own:
        copy.start()

    pl.semaphore_wait(barrier, CTX)

    sends = []

    def send(*args):
        copy = remote(*args)
        copy.start()
        sends.append(copy)

    near = [dev(p, 1 - a, s), dev(p, 1 - a, 1 - s), mate]
    far = [dev(q, 1 - a, s), dev(q, 1 - a, 1 - s), dev(q, a, s), dev(q, a, 1 - s)]
    for n, to in enumerate(far + near):
        send(a_h.at[:, lanes(to, FEAT)], abuf.at[me], a_s.at[n], a_r.at[me], to)
    k_out = []
    for n, to in enumerate(far):
        k_out.append(remote(k_h.at[:, lanes(lax.rem(to, 4), HD)], kbuf.at[mine], k_s.at[n], k_r.at[me], to))

    @pl.when(p == 0)
    def _():
        for copy in k_out:
            copy.start()

    for n, to in enumerate(near):
        send(k_h.at[:, lanes(lax.rem(to, 4), HD)], kbuf.at[mine], k_s.at[4 + n], k_r.at[me], to)
    for n, to in enumerate(near):
        send(q_h.at[:, lanes(lax.rem(to, 4), GROUP * HD)], qbuf.at[here], q_s.at[n], q_r.at[e], to)
    own[0].wait()
    for x, swap in ((p, 0), (q, 1)):
        rows = lanes(x, HALF)
        for m in range(4):
            j = 4 * x + m
            arrived(abuf.at[j], a_r.at[j])
            product = dot(abuf[j], wv[...])
            for h in range(4):
                part[h, lanes(j, ROWS), :] = product[:, h * HD:(h + 1) * HD]
            if m % 2:
                quarter = lanes(2 * x + m // 2, 2 * ROWS)
                for b in range(2):
                    n = 4 * swap + 2 * (m // 2) + b
                    pout[b, quarter, :] = part[2 * b + 1 - s, quarter, :].astype(BF16)
                    send(pout.at[b, quarter], pin.at[b, quarter], p_s.at[n], p_r.at[n], mate)
        for m in range(4):
            j = 4 * x + m
            ft[:, lanes(j, ROWS)] = abuf[j].T
        for m in range(2):
            quarter = lanes(2 * x + m, 2 * ROWS)
            for b in range(2):
                n = 4 * swap + 2 * m + b
                arrived(pin.at[b, quarter], p_r.at[n])
                sums[x, b, m * 2 * ROWS:(m + 1) * 2 * ROWS, :] = (
                    part[2 * b + s, quarter, :] + pin[b, quarter, :].astype(F32)
                ).astype(BF16)
        if swap == 0:
            send(sums.at[p, 1 - a], rbuf.at[i], r_s.at[0], r_r.at[i], dev(p, 1 - a, s))
        else:
            send(sums.at[q, 1 - a], rbuf.at[i], r_s.at[1], r_r.at[i], dev(q, 1 - a, s))
            send(sums.at[q, a], rbuf.at[i], r_s.at[2], r_r.at[i], dev(q, a, s))

    chunk = [0]

    def fill(n):
        for _ in range(n):
            rows = pl.ds(chunk[0] * ROWS, ROWS)
            send(w_h.at[rows], wp_out.at[rows], w_s.at[chunk[0]], w_r.at[chunk[0]], me, peer)
            chunk[0] += 1

    for n, to in enumerate(near):
        send(t_h.at[:, lanes(lax.rem(to, 4), GROUP * HD)], tbuf.at[here], t_s.at[n], t_r.at[e], to)
    fill(FILL[0])

    for n in range(4):
        rows = pl.ds(n * ROWS, ROWS)
        arrived(qbuf.at[rows], q_r.at[n])
    later = lax.broadcasted_iota(jnp.int32, (QB, QB), 0) > lax.broadcasted_iota(jnp.int32, (QB, QB), 1)

    def softmax(base):
        def head(g, carry):
            for b in range(HALF // QB):
                upto = base + (b + 1) * QB
                scores = dot_nt(kbuf[:upto, :], qbuf[b * QB:(b + 1) * QB, lanes(g, HD)])
                edge = jnp.where(later, -jnp.inf, scores[upto - QB:, :])
                scores = jnp.concatenate((scores[:upto - QB, :], edge), axis=0) if upto > QB else edge
                highest = jnp.max(scores, axis=0, keepdims=True)
                raised = jnp.exp2((scores - highest) * (HD ** -0.5 * LOG2E))
                share = 1.0 / jnp.sum(raised, axis=0, keepdims=True)
                cols = lanes(2 * g + b, QB)
                pt[:upto, cols] = (raised * share).astype(BF16)
                if upto < base + HALF:
                    pt[upto:base + HALF, cols] = jnp.zeros((base + HALF - upto, QB), BF16)
            return carry

        lax.fori_loop(0, GROUP, head, 0)

    for j in range(4):
        arrived(kbuf.at[pl.ds(j * ROWS, ROWS)], k_r.at[j])

    @pl.when(p == 0)
    def _():
        softmax(0)

    @pl.when(p == 1)
    def _():
        for j in range(4, CTX):
            arrived(kbuf.at[pl.ds(j * ROWS, ROWS)], k_r.at[j])
        softmax(HALF)

    for other in (2 * p + 1 - a, 2 * q + a, 2 * q + 1 - a):
        arrived(rbuf.at[other], r_r.at[other])
    for m in range(2):
        rows = slice(m * 2 * ROWS, (m + 1) * 2 * ROWS)
        quarter = lanes(2 * p + m, 2 * ROWS)
        total = part[e, quarter, :] + pin[a, quarter, :].astype(F32)
        for other in (2 * p + 1 - a, 2 * q + a, 2 * q + 1 - a):
            total = total + rbuf[other, rows, :].astype(F32)
        v[p, rows, :] = (total * D ** -0.5).astype(BF16)
    onward = remote(v.at[0], v.at[0], v_s.at[0], v_r.at[0], dev(1, a, s))

    @pl.when(p == 0)
    def _():
        onward.start()

    fill(FILL[1])
    vt[:, lanes(p, HALF)] = v[p].T
    for n in range(4):
        rows = pl.ds(n * ROWS, ROWS)
        arrived(tbuf.at[rows], t_r.at[n])

    def attend(base):
        def head(g, carry):
            for b in range(HALF // QB):
                upto = base + (b + 1) * QB
                n = lanes(2 * g + b, QB)
                attended = dot(vt[:, :upto], pt[:upto, n]).T
                wanted = tbuf[b * QB:(b + 1) * QB, lanes(g, HD)].astype(F32)
                cot[n, :] = (LOSS * (attended - wanted)).astype(BF16)
            return carry

        lax.fori_loop(0, GROUP, head, 0)

    @pl.when(p == 0)
    def _():
        attend(0)
        terms = dot(pt[:HALF, :], cot[...])
        arrived(trecv, c_r.at[0])
        vc[e, :HALF, :] = (terms + trecv[...].astype(F32)).astype(BF16)

    back = remote(cross, trecv, c_s.at[0], c_r.at[0], dev(0, a, s))

    @pl.when(p == 1)
    def _():
        arrived(v.at[0], v_r.at[0])
        vt[:, :HALF] = v[0].T
        attend(HALF)
        cross[...] = dot(pt[:HALF, :], cot[...]).astype(BF16)
        back.start()
        vc[e, HALF:, :] = dot(pt[HALF:, :], cot[...]).astype(BF16)

    def block(x, aa, ss):
        return vc.at[2 * aa + ss, lanes(x, HALF)]

    send(block(p, a, s), block(p, a, s), g_s.at[0], g_r.at[i], dev(q, a, s))
    send(block(p, a, s), block(p, a, s), g_s.at[1], g_r.at[i], dev(p, 1 - a, s))
    send(block(p, a, s), block(p, a, s), m_s.at[0], m_r.at[i], mate)
    fill(FILL[2])

    own[5].wait()
    own[6].wait()

    kept = []

    def gradient(n, h):
        cols = lanes(h, HD)
        grad = dot(ft[...], vc[h]) * D ** -0.5
        stepped = trv[:, cols].astype(F32) + grad - ogv[:, cols].astype(F32)
        th[h] = stepped
        th16[h] = stepped.astype(BF16)
        send(th16.at[h], thp_out.at[:, cols], x_s.at[n], x_r.at[n], me, peer)
        keep = pltpu.make_async_copy(th.at[h], th_out.at[:, cols], loc.at[3 + n])
        keep.start()
        kept.append(keep)

    def landed(x, aa):
        arrived(block(x, aa, s), g_r.at[2 * x + aa])

    def passed(x, aa):
        arrived(block(x, aa, 1 - s), m_r.at[2 * x + aa])

    def forward(n, x, aa):
        send(block(x, aa, s), block(x, aa, s), m_s.at[n], m_r.at[2 * x + aa], mate)

    landed(q, a)
    send(block(q, a, s), block(q, a, s), g_s.at[2], g_r.at[2 * q + a], dev(p, 1 - a, s))
    forward(1, q, a)
    gradient(0, e)
    landed(p, 1 - a)
    forward(2, p, 1 - a)
    passed(p, a)
    passed(q, a)
    gradient(1, 2 * a + 1 - s)
    landed(q, 1 - a)
    forward(3, q, 1 - a)
    gradient(2, 2 * (1 - a) + s)
    passed(p, 1 - a)
    passed(q, 1 - a)
    gradient(3, 2 * (1 - a) + 1 - s)
    fill(FILL[3])

    for n in range(4):
        rows = pl.ds(n * ROWS, ROWS)
        arrived(wp_out.at[rows], w_r.at[n])
    for n, h in enumerate((e, 2 * a + 1 - s, 2 * (1 - a) + s, 2 * (1 - a) + 1 - s)):
        kept[n].wait()
        arrived(thp_out.at[:, lanes(h, HD)], x_r.at[n])
    for copy in sends:
        copy.wait_send()

    @pl.when(p == 0)
    def _():
        onward.wait_send()
        for copy in k_out:
            copy.wait_send()

    @pl.when(p == 1)
    def _():
        back.wait_send()


def local(activations, queries, key_states, targets, value_weight, tracker, old_gradient):
    dma = lambda n: pltpu.SemaphoreType.DMA((n,))
    half = jax.ShapeDtypeStruct((FEAT, COLS), BF16)
    th, peer_th, peer_weight = pl.pallas_call(
        kernel,
        out_shape=(jax.ShapeDtypeStruct((FEAT, COLS), F32), half, half),
        in_specs=[pl.BlockSpec(memory_space=pl.ANY)] * 7,
        out_specs=(pl.BlockSpec(memory_space=pl.ANY),) * 3,
        scratch_shapes=[
            pltpu.VMEM((CTX, ROWS, FEAT), BF16),
            pltpu.VMEM((HALF, GROUP * HD), BF16),
            pltpu.VMEM((SEQ, HD), BF16),
            pltpu.VMEM((HALF, GROUP * HD), BF16),
            pltpu.VMEM((FEAT, COLS), BF16),
            pltpu.VMEM((FEAT, COLS), BF16),
            pltpu.VMEM((FEAT, COLS), BF16),
            pltpu.VMEM((FEAT, SEQ), BF16),
            pltpu.VMEM((4, SEQ, HD), F32),
            pltpu.VMEM((2, SEQ, HD), BF16),
            pltpu.VMEM((2, SEQ, HD), BF16),
            pltpu.VMEM((2, 2, HALF, HD), BF16),
            pltpu.VMEM((CHIPS, HALF, HD), BF16),
            pltpu.VMEM((2, HALF, HD), BF16),
            pltpu.VMEM((HD, SEQ), BF16),
            pltpu.VMEM((SEQ, GROUP * HALF), BF16),
            pltpu.VMEM((GROUP * HALF, HD), BF16),
            pltpu.VMEM((HALF, HD), BF16),
            pltpu.VMEM((HALF, HD), BF16),
            pltpu.VMEM((4, SEQ, HD), BF16),
            pltpu.VMEM((4, FEAT, HD), F32),
            pltpu.VMEM((4, FEAT, HD), BF16),
            dma(7), dma(8), dma(3), dma(4), dma(7), dma(8), dma(3), dma(4),
            dma(4), dma(4), dma(8), dma(8), dma(3), dma(4),
            dma(1), dma(1), dma(1), dma(1), dma(3), dma(4), dma(4), dma(4), dma(4), dma(4), dma(7),
        ],
        compiler_params=pltpu.CompilerParams(
            collective_id=0, has_side_effects=True, vmem_limit_bytes=56 * 1024 * 1024
        ),
    )(
        activations[0], queries[0], key_states[0], targets[0],
        value_weight[0], tracker[0], old_gradient[0],
    )
    mixed = (th + peer_th.astype(F32)) * 0.5
    weights = (value_weight[0].astype(F32) + peer_weight.astype(F32)) * 0.5
    return (weights - STEP * mixed).astype(BF16)[None], mixed.astype(BF16)[None]


def solution(mesh):
    spec = P("rep", "ctx", None)
    return jax.shard_map(
        local, mesh=mesh, in_specs=(spec,) * 7, out_specs=(spec, spec), check_vma=False
    )
```
